32 devices in a mesh: disp: 2 (over core), rows: 16 (over z, y, x).
Axes of the slice: x: 2, y: 2, z: 4, core: 2. Of those that a mesh axis runs over, the one named last changes fastest.
Arguments:
- left_features: bfloat16 [320, 32, 256], P(None, 'rows'), may hold values from -6 to 6
- right_features: bfloat16 [320, 32, 256], P(None, 'rows'), may hold values from -6 to 6
- conv_first: bfloat16 [32, 40, 3, 3, 3], replicated, may hold values from -0.375 to 0.375
- conv_second: bfloat16 [32, 32, 3, 3, 3], replicated, may hold values from -0.4375 to 0.4375
- projection: float32 [32], replicated, may hold values from -0.5 to 0.5
Outputs:
- logits: float32 [32, 48, 256], P('rows', 'disp')
- disparity: float32 [32, 256], P('rows')
The draws below stay inside these ranges and needn't reach their ends.
All inputs are finite; a program needn't handle non-finite values.
Results may differ from the reference program's by a relative error of at most 0.0044.
Values may be sent and summed in bfloat16 or wider, within the bound.
A program may use at most 64 MiB of HBM per device.

```python
import jax
import jax.numpy as jnp
from jax import lax

C = 320
G = 40
CH = 32
ROWS_DEV = 2
W = 256
DISP = 48
H = 32


def block_scale(key, dims, split, smallest, top_value):
    factor_of, own = 1.0, jax.random.fold_in(key, 6)
    for dim, blocks in split:
        steps = jnp.exp(jax.random.uniform(jax.random.fold_in(own, dim), (blocks,), jnp.float32, smallest / len(split), top_value / len(split)))
        factor_of = factor_of * jnp.repeat(steps, dims[dim] // blocks).reshape([-1 if axis == dim else 1 for axis in range(len(dims))])
    return factor_of


def normal_values(own_key, dims, scale, limit, cuts=(), kind=jnp.bfloat16):
    drawn = jax.random.normal(own_key, dims, jnp.float32) * scale
    if len(cuts) > 0:
        drawn = block_scale(own_key, dims, cuts, -0.22, 0.18) * drawn
    return jnp.clip(drawn, min=-limit, max=limit).astype(kind)


def setup_inputs(seed: int = 0) -> dict:
    seeds = jax.random.split(jax.random.key(seed), 6)
    left_features = normal_values(seeds[0], (C, H, W), 1.5, 6.0, ((1, 16),))
    right_features = normal_values(seeds[1], (C, H, W), 1.5, 6.0, ((1, 16),))
    conv_first = normal_values(seeds[2], (CH, G, 3, 3, 3), (27 * G // 4) ** -0.5, 0.375)
    conv_second = normal_values(seeds[3], (CH, CH, 3, 3, 3), (27 * CH // 4) ** -0.5, 0.4375)
    projection = normal_values(seeds[4], (CH,), (CH * 4) ** -0.5, 0.5, (), jnp.float32)
    return dict(left_features=left_features, right_features=right_features, conv_first=conv_first, conv_second=conv_second, projection=projection)


def correlate(left_rows, right_rows, first_plane, count):
    right_padded = jnp.pad(right_rows, ((0, 0), (0, 0), (DISP + 2, 2)))
    row_count = left_rows.shape[1]
    left_wide = left_rows.astype(jnp.float32)

    def one_plane(offset):
        plane_id = (first_plane + offset).astype(jnp.int32)
        start = (DISP + 2 - plane_id).astype(jnp.int32)
        shifted = lax.dynamic_slice_in_dim(right_padded, start, W, 2).astype(jnp.float32)
        product = (left_wide * shifted).reshape(G, C // G, row_count, W)
        grouped = jnp.sum(product, axis=1) / (C // G)
        inside_range = (plane_id >= 0) & (plane_id < DISP)
        return jnp.where(inside_range, grouped, jnp.zeros_like(grouped))

    stacked = lax.map(one_plane, jnp.arange(count, dtype=jnp.int32))
    return jnp.transpose(stacked, (1, 2, 0, 3)).astype(jnp.bfloat16)


def convolve(volume, kernel):
    result = lax.conv_general_dilated(volume.astype(jnp.float32)[None], kernel.astype(jnp.float32), (1, 1, 1), "VALID", precision=lax.Precision.HIGHEST)
    return result[0]


def reference(left_features, right_features, conv_first, conv_second, projection):
    left_padded = jnp.pad(left_features, ((0, 0), (2, 2), (0, 0)))
    right_padded = jnp.pad(right_features, ((0, 0), (2, 2), (0, 0)))

    def one_block(block_id):
        first_row = (block_id * ROWS_DEV).astype(jnp.int32)
        left_rows = lax.dynamic_slice_in_dim(left_padded, first_row, ROWS_DEV + 4, 1)
        right_rows = lax.dynamic_slice_in_dim(right_padded, first_row, ROWS_DEV + 4, 1)
        cost = correlate(left_rows, right_rows, jnp.int32(-1), DISP + 2)
        cost = jnp.pad(cost, ((0, 0), (0, 0), (0, 0), (1, 1)))
        first_out = convolve(cost, conv_first)
        row_ids = first_row - 1 + jnp.arange(ROWS_DEV + 2, dtype=jnp.int32)
        row_inside = (row_ids >= 0) & (row_ids < H)
        hidden = jnp.where(row_inside[None, :, None, None], jnp.maximum(first_out, 0.0), 0.0).astype(jnp.bfloat16)
        hidden_padded = jnp.pad(hidden, ((0, 0), (0, 0), (1, 1), (1, 1)))
        second_out = convolve(hidden_padded, conv_second)
        refined = jnp.maximum(second_out, 0.0) + hidden[:, 1:-1].astype(jnp.float32)
        return jnp.einsum("o,oypx->ypx", projection.astype(jnp.float32), refined, precision=lax.Precision.HIGHEST)

    blocks = lax.map(one_block, jnp.arange(H // ROWS_DEV, dtype=jnp.int32))
    logits = blocks.reshape(H, DISP, W)
    weights = jnp.exp(logits)
    plane_values = jnp.arange(DISP, dtype=jnp.float32)
    total = jnp.sum(weights, axis=1)
    weighted = jnp.sum(weights * plane_values[None, :, None], axis=1)
    disparity = weighted / total / DISP
    return logits, disparity
```

```python
import functools

import jax
import jax.numpy as jnp
from jax import lax
from jax.experimental import pallas as pl
from jax.experimental.pallas import tpu as pltpu
from jax.sharding import PartitionSpec as P

DPL_DEV = 24
HALO = 2
INNER = 4
CHUNK = 16
VMEM_BYTES = 24 << 20
MESH = pl.DeviceIdType.MESH


def sum_taps(z, m, lane, width):
    low = jnp.where(lane == 0, 0.0, pltpu.roll(z[:m], 1, 1))
    high = jnp.where(lane == width - 1, 0.0, pltpu.roll(z[2 * m:], width - 1, 1))
    return low + z[m:2 * m] + high


def body(dims, left_ref, right_ref, k1_ref, k2_ref, proj_ref, logits_ref, disparity_ref,
         pair, far, cost, hidden, shifted, inside, w1, w2, sums, send_sems, recv_sems, sum_send, sum_recv):
    per, groups, rows, channels, width, planes, disp_count, row_count = dims
    total = planes * disp_count
    ext_rows = rows + 2 * HALO
    hid_rows = rows + 2
    slab = ext_rows * groups
    hslab = hid_rows * channels
    half_rows = hid_rows // 2
    half_slab = (half_rows + 2) * groups
    half_hslab = half_rows * channels
    cost_planes = planes + 4
    chunks = rows * groups // CHUNK
    disp = lax.axis_index("disp")
    row = lax.axis_index("rows")
    odd = lax.rem(row, 2)
    half = lax.rem(disp, 2)
    other_core = disp + 1 - 2 * half
    partner = row + 1 - 2 * odd
    target = row + 2 - 4 * odd
    source = row - 2 + 4 * odd
    has_target = (target >= 0) & (target < row_count)
    has_source = (source >= 0) & (source < row_count)
    first_plane = disp * planes
    base = first_plane - 2
    base_shift = lax.rem(base + width, width)

    barrier = pltpu.get_barrier_semaphore()

    def greet(d, r):
        pl.semaphore_signal(barrier, inc=1, device_id=(d, r), device_id_type=MESH)

    greet(disp, partner)
    for step in range(1, disp_count):
        greet(lax.rem(disp + step, disp_count), row)

    @pl.when(has_target)
    def _():
        greet(disp, target)

    @pl.when(has_source)
    def _():
        greet(disp, source)

    pl.semaphore_wait(barrier, disp_count + has_target.astype(jnp.int32) + has_source.astype(jnp.int32))

    def rows_of(k):
        return pl.ds(pl.multiple_of(k * CHUNK, CHUNK), CHUNK)

    def copy(kind, k, src, dst, device):
        return pltpu.make_async_remote_copy(
            src_ref=src.at[:, rows_of(k), :],
            dst_ref=dst.at[half, :, rows_of(k), :],
            send_sem=send_sems.at[kind, k],
            recv_sem=recv_sems.at[kind, k],
            device_id=device,
            device_id_type=MESH,
        )

    def to_partner(k, src=left_ref):
        return copy(0, k, src, pair, (disp, partner))

    def pair_to_core(k):
        return copy(1, k, pair.at[half], pair, (other_core, row))

    def pair_to_target(k):
        return copy(2, k, pair.at[half], far, (disp, target))

    def far_to_core(k):
        return copy(3, k, far.at[half], far, (other_core, row))

    for side, src in enumerate((left_ref, right_ref)):
        @pl.when(half == side)
        def _():
            for k in range(chunks):
                to_partner(k, src).start()

    w1[...] = jnp.zeros_like(w1)
    w2[...] = jnp.zeros_like(w2)
    for a in range(3):
        for b in range(3):
            for e in range(3):
                tap = k1_ref[a, b, e]
                for y in range(half_rows):
                    at = (e * half_rows + y) * channels
                    to = b * half_slab + (y + a) * groups
                    w1[at:at + channels, to:to + groups] = tap
                tap = k2_ref[a, b, e]
                for pd in range(2):
                    for y in range(rows):
                        at = ((e * 2 + pd) * rows + y) * channels
                        to = (b + pd) * hslab + (y + a) * channels
                        w2[at:at + channels, to:to + channels] = tap

    lane = lax.broadcasted_iota(jnp.int32, (CHUNK, width), 1)

    for d in range(cost_planes):
        plane = base + d
        keep = (lane >= plane) & (plane >= 0) & (plane < total)
        inside[d] = jnp.where(keep, 1.0 / per, 0.0).astype(jnp.bfloat16)

    def correlate(lref, rref, slab_row, k):
        at = rows_of(k)
        for j in range(per):
            r = pltpu.roll(rref[j, at, :], base_shift, 1)
            shifted[0, j] = r.astype(jnp.float32)
            for d1 in range(1, INNER):
                shifted[d1, j] = pltpu.roll(r, d1, 1).astype(jnp.float32)
        for d2 in range(cost_planes // INNER):
            back = d2 * INNER
            left = []
            for j in range(per):
                value = lref[j, at, :]
                value = pltpu.roll(value, width - back, 1) if back else value
                left.append(value.astype(jnp.float32))
            for d1 in range(INNER):
                terms = [left[j] * shifted[d1, j] for j in range(per)]
                while len(terms) > 1:
                    terms = [x + y for x, y in zip(terms[::2], terms[1::2])]
                acc = terms[0].astype(jnp.bfloat16)
                acc = pltpu.roll(acc, back, 1) if back else acc
                start = pl.multiple_of((back + d1) * slab + slab_row + k * CHUNK, CHUNK)
                cost[pl.ds(start, CHUNK), :] = acc * inside[back + d1]

    pair_row = (1 - odd) * (HALO + rows) * groups
    far_row = odd * (HALO + rows) * groups

    def own_step(k, carry):
        correlate(left_ref, right_ref, HALO * groups, k)
        to_partner(k).wait_recv()
        pair_to_core(k).start()

        @pl.when(has_target)
        def _():
            pair_to_target(k).start()

        return carry

    lax.fori_loop(0, chunks, own_step, 0)

    def pair_step(k, carry):
        pair_to_core(k).wait_recv()
        correlate(pair.at[0], pair.at[1], pair_row, k)
        return carry

    lax.fori_loop(0, chunks, pair_step, 0)

    hlane = lax.broadcasted_iota(jnp.int32, (half_hslab, width), 1)
    top = jnp.where(row > 0, 1.0, 0.0)
    bottom = jnp.where(row < row_count - 1, 1.0, 0.0)

    def first(p, low):
        z = jnp.concatenate([
            cost[pl.ds(pl.multiple_of((p + b) * slab + low * half_rows * groups, CHUNK), half_slab), :]
            for b in range(3)
        ], axis=0)
        z = jnp.dot(w1[...], z, preferred_element_type=jnp.float32)
        h = jnp.maximum(sum_taps(z, half_hslab, hlane, width), 0.0)
        plane = p + first_plane - 1
        valid = jnp.where((plane >= 0) & (plane < total), 1.0, 0.0)
        for y in range(half_rows):
            edge = valid
            if y == 0:
                edge = edge * jnp.where(low == 0, top, 1.0)
            if y == half_rows - 1:
                edge = edge * jnp.where(low == 1, bottom, 1.0)
            at = pl.ds(pl.multiple_of(p * hslab + low * half_hslab + y * channels, CHUNK), channels)
            hidden[at, :] = (h[y * channels:(y + 1) * channels] * edge).astype(jnp.bfloat16)

    def first_step(low):
        def one_plane(p, carry):
            first(p, low)
            return carry
        return one_plane

    lax.fori_loop(0, planes + 2, first_step(1 - odd), 0, unroll=planes + 2)

    def far_step(k, carry):
        @pl.when(has_source)
        def _():
            pair_to_target(k).wait_recv()
            far_to_core(k).start()

        @pl.when(has_source)
        def _():
            far_to_core(k).wait_recv()
            correlate(far.at[0], far.at[1], far_row, k)

        return carry

    lax.fori_loop(0, chunks, far_step, 0)

    @pl.when(jnp.logical_not(has_source))
    def _():
        def clear(p, carry):
            start = pl.multiple_of(p * slab + far_row, CHUNK)
            cost[pl.ds(start, HALO * groups), :] = jnp.zeros((HALO * groups, width), jnp.bfloat16)
            return carry

        lax.fori_loop(0, cost_planes, clear, 0)

    lax.fori_loop(0, planes + 2, first_step(odd), 0, unroll=planes + 2)

    m2 = rows * channels
    olane = lax.broadcasted_iota(jnp.int32, (2 * m2, width), 1)
    diagonal = lax.broadcasted_iota(jnp.int32, (channels, channels), 0) == lax.broadcasted_iota(
        jnp.int32, (channels, channels), 1)
    proj = jnp.sum(jnp.where(diagonal, proj_ref[...], 0.0), axis=1, keepdims=True)

    def second(t, carry):
        at = pl.ds(pl.multiple_of(t * 2 * hslab, CHUNK), 4 * hslab)
        z = jnp.dot(w2[...], hidden[at, :], preferred_element_type=jnp.float32)
        out = jnp.maximum(sum_taps(z, 2 * m2, olane, width), 0.0)
        for pd in range(2):
            start = pl.multiple_of((t * 2 + pd + 1) * hslab + channels, CHUNK)
            for y in range(rows):
                centre = hidden[pl.ds(start + y * channels, channels), :].astype(jnp.float32)
                lo = pd * m2 + y * channels
                refined = (out[lo:lo + channels] + centre) * proj
                logits_ref[y, pl.ds(t * 2 + pd, 1), :] = jnp.sum(refined, axis=0, keepdims=True)
        return carry

    lax.fori_loop(0, planes // 2, second, 0, unroll=planes // 2)

    weights = jnp.exp(logits_ref[...])
    ids = lax.broadcasted_iota(jnp.int32, weights.shape, 1) + first_plane
    sums[disp, 0] = jnp.sum(weights, axis=1)
    sums[disp, 1] = jnp.sum(weights * ids.astype(jnp.float32), axis=1)

    def share(step):
        return pltpu.make_async_remote_copy(
            src_ref=sums.at[disp],
            dst_ref=sums.at[disp],
            send_sem=sum_send.at[step],
            recv_sem=sum_recv.at[step],
            device_id=(lax.rem(disp + step, disp_count), row),
            device_id_type=MESH,
        )

    for step in range(1, disp_count):
        share(step).start()
    for k in range(chunks):
        to_partner(k).wait_send()
        pair_to_core(k).wait_send()

        @pl.when(has_target)
        def _():
            pair_to_target(k).wait_send()

        @pl.when(has_source)
        def _():
            far_to_core(k).wait_send()

    for step in range(1, disp_count):
        share(step).wait()
    both = sums[0]
    for d in range(1, disp_count):
        both = both + sums[d]
    disparity_ref[...] = both[1] / both[0] / total


def per_device(left_features, right_features, conv_first, conv_second, projection):
    disp_count = lax.axis_size("disp")
    row_count = lax.axis_size("rows")
    planes = DPL_DEV
    features, rows, width = left_features.shape
    channels, groups = conv_first.shape[:2]
    per = features // groups

    def arrange(v):
        return v.reshape(groups, per, rows, width).transpose(1, 2, 0, 3).reshape(per, rows * groups, width)

    left, right = arrange(left_features), arrange(right_features)
    both = (2,) + left.shape
    k1 = conv_first.transpose(2, 3, 4, 0, 1)
    k2 = conv_second.transpose(2, 3, 4, 0, 1)
    ext_rows, hid_rows = rows + 2 * HALO, rows + 2
    slab, hslab = ext_rows * groups, hid_rows * channels
    chunks = rows * groups // CHUNK
    dims = (per, groups, rows, channels, width, planes, disp_count, row_count)
    return pl.pallas_call(
        functools.partial(body, dims),
        out_shape=(
            jax.ShapeDtypeStruct((rows, planes, width), jnp.float32),
            jax.ShapeDtypeStruct((rows, width), jnp.float32),
        ),
        in_specs=[pl.BlockSpec(memory_space=pltpu.VMEM)] * 5,
        out_specs=(pl.BlockSpec(memory_space=pltpu.VMEM),) * 2,
        scratch_shapes=[
            pltpu.VMEM(both, left.dtype),
            pltpu.VMEM(both, left.dtype),
            pltpu.VMEM(((planes + 4) * slab, width), jnp.bfloat16),
            pltpu.VMEM(((planes + 2) * hslab, width), jnp.bfloat16),
            pltpu.VMEM((INNER, per, CHUNK, width), jnp.float32),
            pltpu.VMEM((planes + 4, CHUNK, width), jnp.bfloat16),
            pltpu.VMEM((3 * hid_rows // 2 * channels, 3 * (hid_rows // 2 + 2) * groups), jnp.bfloat16),
            pltpu.VMEM((3 * 2 * rows * channels, 4 * hslab), jnp.bfloat16),
            pltpu.VMEM((disp_count, 2, rows, width), jnp.float32),
            pltpu.SemaphoreType.DMA((4, chunks)),
            pltpu.SemaphoreType.DMA((4, chunks)),
            pltpu.SemaphoreType.DMA((disp_count,)),
            pltpu.SemaphoreType.DMA((disp_count,)),
        ],
        compiler_params=pltpu.CompilerParams(collective_id=0, has_side_effects=True, vmem_limit_bytes=VMEM_BYTES),
    )(left, right, k1, k2, projection[None])


def solution(mesh):
    return jax.shard_map(
        per_device,
        mesh=mesh,
        in_specs=(P(None, "rows", None), P(None, "rows", None), P(), P(), P()),
        out_specs=(P("rows", "disp", None), P("rows", None)),
        check_vma=False,
    )
```

```python
import functools

import jax
import jax.numpy as jnp
from jax import lax
from jax.experimental import pallas as pl
from jax.experimental.pallas import tpu as pltpu
from jax.sharding import PartitionSpec as P

DPL_DEV = 24
HALO = 2
INNER = 7
CHUNK = 16
PIECES = 1
VMEM_BYTES = 28 << 20
MESH = pl.DeviceIdType.MESH


def sum_taps(z, m, lane, width):
    low = jnp.where(lane == 0, 0.0, pltpu.roll(z[:m], 1, 1))
    high = jnp.where(lane == width - 1, 0.0, pltpu.roll(z[2 * m:], width - 1, 1))
    return low + z[m:2 * m] + high


def body(dims, left_ref, right_ref, k1_hbm, k2_hbm, proj_hbm, logits_ref, disparity_ref,
         k1_ref, k2_ref, proj_ref, pair, far, cost, hidden, shifted, shifts, inside, w1, w2, sums,
         load_sems, send_sems, recv_sems, sum_send, sum_recv):
    per, groups, rows, channels, width, planes, disp_count, row_count = dims
    total = planes * disp_count
    hid_rows = rows + 2
    block = rows * groups
    hslab = hid_rows * channels
    half_rows = hid_rows // 2
    half_hslab = half_rows * channels
    cost_planes = planes + 4
    source_rows = cost_planes * block
    chunks = block // CHUNK
    disp = lax.axis_index("disp")
    row = lax.axis_index("rows")
    odd = lax.rem(row, 2)
    half = lax.rem(disp, 2)
    other_core = disp + 1 - 2 * half
    partner = row + 1 - 2 * odd
    target = row + 2 - 4 * odd
    source = row - 2 + 4 * odd
    has_target = (target >= 0) & (target < row_count)
    has_source = (source >= 0) & (source < row_count)
    first_plane = disp * planes
    base = first_plane - 2

    load1 = pltpu.make_async_copy(k1_hbm, k1_ref, load_sems.at[0])
    load2 = pltpu.make_async_copy(k2_hbm, k2_ref, load_sems.at[1])
    load3 = pltpu.make_async_copy(proj_hbm, proj_ref, load_sems.at[2])
    load1.start()
    load2.start()
    load3.start()

    barrier = pltpu.get_barrier_semaphore()

    def greet(d, r):
        pl.semaphore_signal(barrier, inc=1, device_id=(d, r), device_id_type=MESH)

    greet(disp, partner)
    for step in range(1, disp_count):
        greet(lax.rem(disp + step, disp_count), row)

    @pl.when(has_source)
    def _():
        greet(disp, source)

    pl.semaphore_wait(barrier, disp_count + has_target.astype(jnp.int32))

    part = per // PIECES

    def copy(kind, q, src, dst, device):
        k, piece = divmod(q, PIECES)
        at, chans = pl.ds(k * CHUNK, CHUNK), pl.ds(piece * part, part)
        return pltpu.make_async_remote_copy(
            src_ref=src.at[chans, at, :],
            dst_ref=dst.at[half, chans, at, :],
            send_sem=send_sems.at[kind, q],
            recv_sem=recv_sems.at[kind, q],
            device_id=device,
            device_id_type=MESH,
        )

    def to_partner(k, src=left_ref):
        return copy(0, k, src, pair, (disp, partner))

    def pair_to_core(k):
        return copy(1, k, pair.at[half], pair, (other_core, row))

    def pair_to_target(k):
        return copy(2, k, pair.at[half], far, (disp, target))

    def far_to_core(k):
        return copy(3, k, far.at[half], far, (other_core, row))

    for side, src in enumerate((left_ref, right_ref)):
        @pl.when(half == side)
        def _():
            for q in range(chunks * PIECES):
                to_partner(q, src).start()

    def forward_pair(k):
        for q in range(k * PIECES, (k + 1) * PIECES):
            to_partner(q).wait_recv()
            pair_to_core(q).start()

            @pl.when(has_target)
            def _():
                pair_to_target(q).start()

    def forward_far(k):
        @pl.when(has_source)
        def _():
            for q in range(k * PIECES, (k + 1) * PIECES):
                pair_to_target(q).wait_recv()
                far_to_core(q).start()

    lane = lax.broadcasted_iota(jnp.int32, (CHUNK, width), 1)
    for d in range(cost_planes):
        plane = base + d
        keep = (lane >= plane) & (plane >= 0) & (plane < total)
        inside[d] = jnp.where(keep, 1.0 / per, 0.0).astype(jnp.bfloat16)

    gap = lax.broadcasted_iota(jnp.int32, (width, width), 1) - lax.broadcasted_iota(jnp.int32, (width, width), 0)
    for d1 in range(INNER):
        by = base + d1
        hit = (gap == by) | (gap == by - width) | (gap == by + width)
        shifts[d1] = jnp.where(hit, 1.0, 0.0).astype(jnp.bfloat16)

    def correlate(lref, rref, slot, k, buf, kind=jnp.bfloat16):
        at = pl.ds(k * CHUNK, CHUNK)
        right = rref[:, at, :].reshape(per * CHUNK, width)
        for d1 in range(INNER):
            moved = jnp.dot(right, shifts[d1], preferred_element_type=jnp.float32)
            shifted[buf, d1] = moved.astype(jnp.bfloat16).reshape(per, CHUNK, width)
        for d2 in range(cost_planes // INNER):
            back = d2 * INNER
            left = []
            for j in range(per):
                value = lref[j, at, :]
                value = pltpu.roll(value, width - back, 1) if back else value
                left.append(value.astype(kind))
            for d1 in range(INNER):
                terms = [left[j] * shifted[buf, d1, j].astype(kind) for j in range(per)]
                while len(terms) > 1:
                    terms = [x + y for x, y in zip(terms[::2], terms[1::2])]
                acc = terms[0].astype(jnp.bfloat16)
                acc = pltpu.roll(acc, back, 1) if back else acc
                start = pl.multiple_of(slot * source_rows + (back + d1) * block + k * CHUNK, CHUNK)
                cost[pl.ds(start, CHUNK), :] = acc * inside[back + d1]

    pair_slot = 2 - 2 * odd
    far_slot = 2 * odd

    def correlate_own(k):
        correlate(left_ref, right_ref, 1, k, k % 2, jnp.float32)

    def correlate_pair(k):
        for q in range(k * PIECES, (k + 1) * PIECES):
            pair_to_core(q).wait_recv()
        correlate(pair.at[0], pair.at[1], pair_slot, k, 0)

    def correlate_far(k):
        @pl.when(has_source)
        def _():
            for q in range(k * PIECES, (k + 1) * PIECES):
                far_to_core(q).wait_recv()
            correlate(far.at[0], far.at[1], far_slot, k, 1)

    for k in range(chunks):
        correlate_own(k)

    def weights():
        w1[...] = jnp.zeros_like(w1)
        w2[...] = jnp.zeros_like(w2)
        load1.wait()
        load2.wait()
        load3.wait()
        for a in range(3):
            for b in range(3):
                for e in range(3):
                    tap = k1_ref[a, b, e]
                    for y in range(half_rows):
                        at = (e * half_rows + y) * channels
                        which, within = divmod(y + a, rows)
                        to = which * 3 * block + b * block + within * groups
                        w1[at:at + channels, to:to + groups] = tap
                    tap = k2_ref[a, b, e]
                    for pd in range(2):
                        for y in range(rows):
                            at = ((e * 2 + pd) * rows + y) * channels
                            to = (b + pd) * hslab + (y + a) * channels
                            w2[at:at + channels, to:to + channels] = tap

    @pl.when(jnp.logical_not(has_source))
    def _():
        def clear(p, carry):
            start = pl.multiple_of(far_slot * source_rows + p * block, CHUNK)
            cost[pl.ds(start, block), :] = jnp.zeros((block, width), jnp.bfloat16)
            return carry

        lax.fori_loop(0, cost_planes, clear, 0)

    hlane = lax.broadcasted_iota(jnp.int32, (half_hslab, width), 1)
    top = jnp.where(row > 0, 1.0, 0.0)
    bottom = jnp.where(row < row_count - 1, 1.0, 0.0)

    def first(p, low):
        z = jnp.concatenate([
            cost[pl.ds(pl.multiple_of((low + s) * source_rows + p * block, CHUNK), 3 * block), :]
            for s in range(2)
        ], axis=0)
        z = jnp.dot(w1[...], z, preferred_element_type=jnp.float32)
        h = jnp.maximum(sum_taps(z, half_hslab, hlane, width), 0.0)
        plane = p + first_plane - 1
        valid = jnp.where((plane >= 0) & (plane < total), 1.0, 0.0)
        for y in range(half_rows):
            edge = valid
            if y == 0:
                edge = edge * jnp.where(low == 0, top, 1.0)
            if y == half_rows - 1:
                edge = edge * jnp.where(low == 1, bottom, 1.0)
            at = pl.ds(pl.multiple_of(p * hslab + low * half_hslab + y * channels, CHUNK), channels)
            hidden[at, :] = (h[y * channels:(y + 1) * channels] * edge).astype(jnp.bfloat16)

    def first_planes(begin, end, low):
        def one_plane(p, carry):
            first(p, low)
            return carry

        lax.fori_loop(begin, end, one_plane, 0, unroll=end - begin)

    for k in range(chunks):
        forward_pair(k)
        if k == 0:
            weights()
        else:
            correlate_pair(k - 1)
    forward_far(0)
    correlate_pair(chunks - 1)
    forward_far(1)
    steps = chunks - 1
    cuts = [(planes + 2) * i // steps for i in range(steps + 1)]
    for i in range(steps):
        first_planes(cuts[i], cuts[i + 1], 1 - odd)
        if i + 2 < chunks:
            forward_far(i + 2)
        correlate_far(i)
    correlate_far(chunks - 1)
    first_planes(0, planes + 2, odd)

    m2 = rows * channels
    olane = lax.broadcasted_iota(jnp.int32, (2 * m2, width), 1)
    diagonal = lax.broadcasted_iota(jnp.int32, (channels, channels), 0) == lax.broadcasted_iota(
        jnp.int32, (channels, channels), 1)
    proj = jnp.sum(jnp.where(diagonal, proj_ref[...], 0.0), axis=1, keepdims=True)

    def second(t, carry):
        at = pl.ds(pl.multiple_of(t * 2 * hslab, CHUNK), 4 * hslab)
        z = jnp.dot(w2[...], hidden[at, :], preferred_element_type=jnp.float32)
        out = jnp.maximum(sum_taps(z, 2 * m2, olane, width), 0.0)
        for pd in range(2):
            start = pl.multiple_of((t * 2 + pd + 1) * hslab + channels, CHUNK)
            for y in range(rows):
                centre = hidden[pl.ds(start + y * channels, channels), :].astype(jnp.float32)
                lo = pd * m2 + y * channels
                refined = (out[lo:lo + channels] + centre) * proj
                logits_ref[y, pl.ds(t * 2 + pd, 1), :] = jnp.sum(refined, axis=0, keepdims=True)
        return carry

    lax.fori_loop(0, planes // 2, second, 0, unroll=planes // 2)

    weights_now = jnp.exp(logits_ref[...])
    ids = lax.broadcasted_iota(jnp.int32, weights_now.shape, 1) + first_plane
    sums[disp, 0] = jnp.sum(weights_now, axis=1)
    sums[disp, 1] = jnp.sum(weights_now * ids.astype(jnp.float32), axis=1)

    def share(step):
        return pltpu.make_async_remote_copy(
            src_ref=sums.at[disp],
            dst_ref=sums.at[disp],
            send_sem=sum_send.at[step],
            recv_sem=sum_recv.at[step],
            device_id=(lax.rem(disp + step, disp_count), row),
            device_id_type=MESH,
        )

    for step in range(1, disp_count):
        share(step).start()
    for k in range(chunks * PIECES):
        to_partner(k).wait_send()
        pair_to_core(k).wait_send()

        @pl.when(has_target)
        def _():
            pair_to_target(k).wait_send()

        @pl.when(has_source)
        def _():
            far_to_core(k).wait_send()

    for step in range(1, disp_count):
        share(step).wait()
    both = sums[0]
    for d in range(1, disp_count):
        both = both + sums[d]
    disparity_ref[...] = both[1] / both[0] / total


def per_device(left_features, right_features, conv_first, conv_second, projection):
    disp_count = lax.axis_size("disp")
    row_count = lax.axis_size("rows")
    planes = DPL_DEV
    features, rows, width = left_features.shape
    channels, groups = conv_first.shape[:2]
    per = features // groups

    def arrange(v):
        return v.reshape(groups, per, rows, width).transpose(1, 2, 0, 3).reshape(per, rows * groups, width)

    left, right = arrange(left_features), arrange(right_features)
    both = (2,) + left.shape
    def in_hbm(v):
        return pltpu.with_memory_space_constraint(v, pltpu.HBM)

    k1 = in_hbm(conv_first.transpose(2, 3, 4, 0, 1))
    k2 = in_hbm(conv_second.transpose(2, 3, 4, 0, 1))
    proj = in_hbm(projection[None])
    hid_rows = rows + 2
    block, hslab = rows * groups, hid_rows * channels
    chunks = block // CHUNK
    dims = (per, groups, rows, channels, width, planes, disp_count, row_count)
    vmem = pl.BlockSpec(memory_space=pltpu.VMEM)
    hbm = pl.BlockSpec(memory_space=pltpu.HBM)
    return pl.pallas_call(
        functools.partial(body, dims),
        out_shape=(
            jax.ShapeDtypeStruct((rows, planes, width), jnp.float32),
            jax.ShapeDtypeStruct((rows, width), jnp.float32),
        ),
        in_specs=[vmem, vmem, hbm, hbm, hbm],
        out_specs=(vmem, vmem),
        scratch_shapes=[
            pltpu.VMEM(k1.shape, k1.dtype),
            pltpu.VMEM(k2.shape, k2.dtype),
            pltpu.VMEM(proj.shape, proj.dtype),
            pltpu.VMEM(both, left.dtype),
            pltpu.VMEM(both, left.dtype),
            pltpu.VMEM((3 * (planes + 4) * block, width), jnp.bfloat16),
            pltpu.VMEM(((planes + 2) * hslab, width), jnp.bfloat16),
            pltpu.VMEM((2, INNER, per, CHUNK, width), jnp.bfloat16),
            pltpu.VMEM((INNER, width, width), jnp.bfloat16),
            pltpu.VMEM((planes + 4, CHUNK, width), jnp.bfloat16),
            pltpu.VMEM((3 * hid_rows // 2 * channels, 6 * block), jnp.bfloat16),
            pltpu.VMEM((3 * 2 * rows * channels, 4 * hslab), jnp.bfloat16),
            pltpu.VMEM((disp_count, 2, rows, width), jnp.float32),
            pltpu.SemaphoreType.DMA((3,)),
            pltpu.SemaphoreType.DMA((4, chunks * PIECES)),
            pltpu.SemaphoreType.DMA((4, chunks * PIECES)),
            pltpu.SemaphoreType.DMA((disp_count,)),
            pltpu.SemaphoreType.DMA((disp_count,)),
        ],
        compiler_params=pltpu.CompilerParams(
            collective_id=0, has_side_effects=True, vmem_limit_bytes=VMEM_BYTES),
    )(left, right, k1, k2, proj)


def solution(mesh):
    return jax.shard_map(
        per_device,
        mesh=mesh,
        in_specs=(P(None, "rows", None), P(None, "rows", None), P(), P(), P()),
        out_specs=(P("rows", "disp", None), P("rows", None)),
        check_vma=False,
    )
```

```python
import functools

import jax
import jax.numpy as jnp
from jax import lax
from jax.experimental import pallas as pl
from jax.experimental.pallas import tpu as pltpu
from jax.sharding import PartitionSpec as P

DPL_DEV = 24
HALO = 2
INNER = 7
CHUNK = 16
PIECES = 1
VMEM_BYTES = 28 << 20
MESH = pl.DeviceIdType.MESH


def sum_taps(z, m, lane, width):
    low = jnp.where(lane == 0, 0.0, pltpu.roll(z[:m], 1, 1))
    high = jnp.where(lane == width - 1, 0.0, pltpu.roll(z[2 * m:], width - 1, 1))
    return low + z[m:2 * m] + high


def body(dims, left_ref, right_ref, k1_hbm, k2_hbm, proj_hbm, logits_ref, disparity_ref,
         k1_ref, k2_ref, proj_ref, pair, far, cost, hidden, shifted, shifts, inside, w1, w2, sums,
         load_sems, send_sems, recv_sems, sum_send, sum_recv):
    per, groups, rows, channels, width, planes, disp_count, row_count = dims
    total = planes * disp_count
    hid_rows = rows + 2
    block = rows * groups
    hslab = hid_rows * channels
    half_rows = hid_rows // 2
    half_hslab = half_rows * channels
    cost_planes = planes + 4
    source_rows = cost_planes * block
    chunks = block // CHUNK
    disp = lax.axis_index("disp")
    row = lax.axis_index("rows")
    odd = lax.rem(row, 2)
    half = lax.rem(disp, 2)
    other_core = disp + 1 - 2 * half
    partner = row + 1 - 2 * odd
    target = row + 2 - 4 * odd
    source = row - 2 + 4 * odd
    has_target = (target >= 0) & (target < row_count)
    has_source = (source >= 0) & (source < row_count)
    first_plane = disp * planes
    base = first_plane - 2

    load1 = pltpu.make_async_copy(k1_hbm, k1_ref, load_sems.at[0])
    load2 = pltpu.make_async_copy(k2_hbm, k2_ref, load_sems.at[1])
    load3 = pltpu.make_async_copy(proj_hbm, proj_ref, load_sems.at[2])
    load1.start()
    load2.start()
    load3.start()

    barrier = pltpu.get_barrier_semaphore()

    def greet(d, r):
        pl.semaphore_signal(barrier, inc=1, device_id=(d, r), device_id_type=MESH)

    greet(disp, partner)
    for step in range(1, disp_count):
        greet(lax.rem(disp + step, disp_count), row)

    @pl.when(has_source)
    def _():
        greet(disp, source)

    pl.semaphore_wait(barrier, disp_count + has_target.astype(jnp.int32))

    part = per // PIECES

    def copy(kind, q, src, dst, device):
        k, piece = divmod(q, PIECES)
        at, chans = pl.ds(k * CHUNK, CHUNK), pl.ds(piece * part, part)
        return pltpu.make_async_remote_copy(
            src_ref=src.at[chans, at, :],
            dst_ref=dst.at[half, chans, at, :],
            send_sem=send_sems.at[kind, q],
            recv_sem=recv_sems.at[kind, q],
            device_id=device,
            device_id_type=MESH,
        )

    def to_partner(k, src=left_ref):
        return copy(0, k, src, pair, (disp, partner))

    def pair_to_core(k):
        return copy(1, k, pair.at[half], pair, (other_core, row))

    def pair_to_target(k):
        return copy(2, k, pair.at[half], far, (disp, target))

    def far_to_core(k):
        return copy(3, k, far.at[half], far, (other_core, row))

    for side, src in enumerate((left_ref, right_ref)):
        @pl.when(half == side)
        def _():
            for q in range(chunks * PIECES):
                to_partner(q, src).start()

    def forward_pair(k):
        for q in range(k * PIECES, (k + 1) * PIECES):
            to_partner(q).wait_recv()

            @pl.when(has_target)
            def _():
                pair_to_target(q).start()

            pair_to_core(q).start()

    def forward_far(k):
        @pl.when(has_source)
        def _():
            for q in range(k * PIECES, (k + 1) * PIECES):
                pair_to_target(q).wait_recv()
                far_to_core(q).start()

    lane = lax.broadcasted_iota(jnp.int32, (CHUNK, width), 1)
    for d in range(cost_planes):
        plane = base + d
        keep = (lane >= plane) & (plane >= 0) & (plane < total)
        inside[d] = jnp.where(keep, 1.0 / per, 0.0).astype(jnp.bfloat16)

    gap = lax.broadcasted_iota(jnp.int32, (width, width), 1) - lax.broadcasted_iota(jnp.int32, (width, width), 0)
    for d1 in range(INNER):
        by = base + d1
        hit = (gap == by) | (gap == by - width) | (gap == by + width)
        shifts[d1] = jnp.where(hit, 1.0, 0.0).astype(jnp.bfloat16)

    def correlate(lref, rref, slot, k, buf, kind=jnp.bfloat16):
        at = pl.ds(k * CHUNK, CHUNK)
        right = rref[:, at, :].reshape(per * CHUNK, width)
        for d1 in range(INNER):
            moved = jnp.dot(right, shifts[d1], preferred_element_type=jnp.float32)
            shifted[buf, d1] = moved.astype(jnp.bfloat16).reshape(per, CHUNK, width)
        for d2 in range(cost_planes // INNER):
            back = d2 * INNER
            left = []
            for j in range(per):
                value = lref[j, at, :]
                value = pltpu.roll(value, width - back, 1) if back else value
                left.append(value.astype(kind))
            for d1 in range(INNER):
                terms = [left[j] * shifted[buf, d1, j].astype(kind) for j in range(per)]
                while len(terms) > 1:
                    terms = [x + y for x, y in zip(terms[::2], terms[1::2])]
                acc = terms[0].astype(jnp.bfloat16)
                acc = pltpu.roll(acc, back, 1) if back else acc
                start = pl.multiple_of(slot * source_rows + (back + d1) * block + k * CHUNK, CHUNK)
                cost[pl.ds(start, CHUNK), :] = acc * inside[back + d1]

    pair_slot = 2 - 2 * odd
    far_slot = 2 * odd

    def correlate_own(k):
        correlate(left_ref, right_ref, 1, k, k % 2, jnp.float32)

    def correlate_pair(k):
        for q in range(k * PIECES, (k + 1) * PIECES):
            pair_to_core(q).wait_recv()
        correlate(pair.at[0], pair.at[1], pair_slot, k, 0)

    def correlate_far(k):
        @pl.when(has_source)
        def _():
            for q in range(k * PIECES, (k + 1) * PIECES):
                far_to_core(q).wait_recv()
            correlate(far.at[0], far.at[1], far_slot, k, 1)

    for k in range(chunks):
        correlate_own(k)

    def weights():
        w1[...] = jnp.zeros_like(w1)
        w2[...] = jnp.zeros_like(w2)
        load1.wait()
        load2.wait()
        load3.wait()
        for a in range(3):
            for b in range(3):
                for e in range(3):
                    tap = k1_ref[a, b, e]
                    for y in range(half_rows):
                        at = (e * half_rows + y) * channels
                        which, within = divmod(y + a, rows)
                        to = which * 3 * block + b * block + within * groups
                        w1[at:at + channels, to:to + groups] = tap
                    tap = k2_ref[a, b, e]
                    for pd in range(2):
                        for y in range(rows):
                            at = ((e * 2 + pd) * rows + y) * channels
                            to = (b + pd) * hslab + (y + a) * channels
                            w2[at:at + channels, to:to + channels] = tap

    @pl.when(jnp.logical_not(has_source))
    def _():
        def clear(p, carry):
            start = pl.multiple_of(far_slot * source_rows + p * block, CHUNK)
            cost[pl.ds(start, block), :] = jnp.zeros((block, width), jnp.bfloat16)
            return carry

        lax.fori_loop(0, cost_planes, clear, 0)

    hlane = lax.broadcasted_iota(jnp.int32, (half_hslab, width), 1)
    top = jnp.where(row > 0, 1.0, 0.0)
    bottom = jnp.where(row < row_count - 1, 1.0, 0.0)

    def first(p, low):
        z = jnp.concatenate([
            cost[pl.ds(pl.multiple_of((low + s) * source_rows + p * block, CHUNK), 3 * block), :]
            for s in range(2)
        ], axis=0)
        z = jnp.dot(w1[...], z, preferred_element_type=jnp.float32)
        h = jnp.maximum(sum_taps(z, half_hslab, hlane, width), 0.0)
        plane = p + first_plane - 1
        valid = jnp.where((plane >= 0) & (plane < total), 1.0, 0.0)
        for y in range(half_rows):
            edge = valid
            if y == 0:
                edge = edge * jnp.where(low == 0, top, 1.0)
            if y == half_rows - 1:
                edge = edge * jnp.where(low == 1, bottom, 1.0)
            at = pl.ds(pl.multiple_of(p * hslab + low * half_hslab + y * channels, CHUNK), channels)
            hidden[at, :] = (h[y * channels:(y + 1) * channels] * edge).astype(jnp.bfloat16)

    def first_planes(begin, end, low):
        def one_plane(p, carry):
            first(p, low)
            return carry

        lax.fori_loop(begin, end, one_plane, 0, unroll=end - begin)

    for k in range(chunks):
        forward_pair(k)
        if k == 0:
            weights()
        else:
            correlate_pair(k - 1)
    forward_far(0)
    correlate_pair(chunks - 1)
    forward_far(1)
    steps = chunks - 1
    cuts = [(planes + 2) * i // steps for i in range(steps + 1)]
    for i in range(steps):
        first_planes(cuts[i], cuts[i + 1], 1 - odd)
        if i + 2 < chunks:
            forward_far(i + 2)
        correlate_far(i)
    correlate_far(chunks - 1)
    first_planes(0, planes + 2, odd)

    m2 = rows * channels
    olane = lax.broadcasted_iota(jnp.int32, (2 * m2, width), 1)
    diagonal = lax.broadcasted_iota(jnp.int32, (channels, channels), 0) == lax.broadcasted_iota(
        jnp.int32, (channels, channels), 1)
    proj = jnp.sum(jnp.where(diagonal, proj_ref[...], 0.0), axis=1, keepdims=True)

    def second(t, carry):
        at = pl.ds(pl.multiple_of(t * 2 * hslab, CHUNK), 4 * hslab)
        z = jnp.dot(w2[...], hidden[at, :], preferred_element_type=jnp.float32)
        out = jnp.maximum(sum_taps(z, 2 * m2, olane, width), 0.0)
        for pd in range(2):
            start = pl.multiple_of((t * 2 + pd + 1) * hslab + channels, CHUNK)
            for y in range(rows):
                centre = hidden[pl.ds(start + y * channels, channels), :].astype(jnp.float32)
                lo = pd * m2 + y * channels
                refined = (out[lo:lo + channels] + centre) * proj
                logits_ref[y, pl.ds(t * 2 + pd, 1), :] = jnp.sum(refined, axis=0, keepdims=True)
        return carry

    lax.fori_loop(0, planes // 2, second, 0, unroll=planes // 2)

    weights_now = jnp.exp(logits_ref[...])
    ids = lax.broadcasted_iota(jnp.int32, weights_now.shape, 1) + first_plane
    sums[disp, 0] = jnp.sum(weights_now, axis=1)
    sums[disp, 1] = jnp.sum(weights_now * ids.astype(jnp.float32), axis=1)

    def share(step):
        return pltpu.make_async_remote_copy(
            src_ref=sums.at[disp],
            dst_ref=sums.at[disp],
            send_sem=sum_send.at[step],
            recv_sem=sum_recv.at[step],
            device_id=(lax.rem(disp + step, disp_count), row),
            device_id_type=MESH,
        )

    for step in range(1, disp_count):
        share(step).start()
    for k in range(chunks * PIECES):
        to_partner(k).wait_send()
        pair_to_core(k).wait_send()

        @pl.when(has_target)
        def _():
            pair_to_target(k).wait_send()

        @pl.when(has_source)
        def _():
            far_to_core(k).wait_send()

    for step in range(1, disp_count):
        share(step).wait()
    both = sums[0]
    for d in range(1, disp_count):
        both = both + sums[d]
    disparity_ref[...] = both[1] / both[0] / total


def emit(logits_in, disparity_in, logits_out, disparity_out):
    logits_out[...] = logits_in[...]
    disparity_out[...] = disparity_in[...]


def per_device(left_features, right_features, conv_first, conv_second, projection):
    disp_count = lax.axis_size("disp")
    row_count = lax.axis_size("rows")
    planes = DPL_DEV
    features, rows, width = left_features.shape
    channels, groups = conv_first.shape[:2]
    per = features // groups

    def arrange(v):
        return v.reshape(groups, per, rows, width).transpose(1, 2, 0, 3).reshape(per, rows * groups, width)

    left, right = arrange(left_features), arrange(right_features)
    both = (2,) + left.shape
    def in_hbm(v):
        return pltpu.with_memory_space_constraint(v, pltpu.HBM)

    k1 = in_hbm(conv_first.transpose(2, 3, 4, 0, 1))
    k2 = in_hbm(conv_second.transpose(2, 3, 4, 0, 1))
    proj = in_hbm(projection[None])
    hid_rows = rows + 2
    block, hslab = rows * groups, hid_rows * channels
    chunks = block // CHUNK
    dims = (per, groups, rows, channels, width, planes, disp_count, row_count)
    vmem = pl.BlockSpec(memory_space=pltpu.VMEM)
    hbm = pl.BlockSpec(memory_space=pltpu.HBM)
    results = (
        jax.ShapeDtypeStruct((rows, planes, width), jnp.float32),
        jax.ShapeDtypeStruct((rows, width), jnp.float32),
    )
    made = pl.pallas_call(
        functools.partial(body, dims),
        out_shape=results,
        in_specs=[vmem, vmem, hbm, hbm, hbm],
        out_specs=(vmem, vmem),
        scratch_shapes=[
            pltpu.VMEM(k1.shape, k1.dtype),
            pltpu.VMEM(k2.shape, k2.dtype),
            pltpu.VMEM(proj.shape, proj.dtype),
            pltpu.VMEM(both, left.dtype),
            pltpu.VMEM(both, left.dtype),
            pltpu.VMEM((3 * (planes + 4) * block, width), jnp.bfloat16),
            pltpu.VMEM(((planes + 2) * hslab, width), jnp.bfloat16),
            pltpu.VMEM((2, INNER, per, CHUNK, width), jnp.bfloat16),
            pltpu.VMEM((INNER, width, width), jnp.bfloat16),
            pltpu.VMEM((planes + 4, CHUNK, width), jnp.bfloat16),
            pltpu.VMEM((3 * hid_rows // 2 * channels, 6 * block), jnp.bfloat16),
            pltpu.VMEM((3 * 2 * rows * channels, 4 * hslab), jnp.bfloat16),
            pltpu.VMEM((disp_count, 2, rows, width), jnp.float32),
            pltpu.SemaphoreType.DMA((3,)),
            pltpu.SemaphoreType.DMA((4, chunks * PIECES)),
            pltpu.SemaphoreType.DMA((4, chunks * PIECES)),
            pltpu.SemaphoreType.DMA((disp_count,)),
            pltpu.SemaphoreType.DMA((disp_count,)),
        ],
        compiler_params=pltpu.CompilerParams(
            collective_id=0, has_side_effects=True, vmem_limit_bytes=VMEM_BYTES),
    )(left, right, k1, k2, proj)
    return pl.pallas_call(
        emit,
        out_shape=results,
        in_specs=[vmem, vmem],
        out_specs=(vmem, vmem),
        compiler_params=pltpu.CompilerParams(vmem_limit_bytes=VMEM_BYTES // 8),
    )(*made)


def solution(mesh):
    return jax.shard_map(
        per_device,
        mesh=mesh,
        in_specs=(P(None, "rows", None), P(None, "rows", None), P(), P(), P()),
        out_specs=(P("rows", "disp", None), P("rows", None)),
        check_vma=False,
    )
```

```python
import functools

import jax
import jax.numpy as jnp
from jax import lax
from jax.experimental import pallas as pl
from jax.experimental.pallas import tpu as pltpu
from jax.sharding import PartitionSpec as P

DPL_DEV = 24
HALO = 2
INNER = 7
CHUNK = 16
PIECES = 1
VMEM_BYTES = 28 << 20
MESH = pl.DeviceIdType.MESH


def sum_taps(z, m, lane, width):
    low = jnp.where(lane == 0, 0.0, pltpu.roll(z[:m], 1, 1))
    high = jnp.where(lane == width - 1, 0.0, pltpu.roll(z[2 * m:], width - 1, 1))
    return low + z[m:2 * m] + high


def body(dims, left_ref, right_ref, k1_hbm, k2_hbm, proj_hbm, logits_ref, disparity_ref,
         k1_ref, k2_ref, proj_ref, pair, far, cost_own, cost_pair, cost_far, hidden, shifted, shifts, inside, w1, w2, sums,
         load_sems, send_sems, recv_sems, sum_send, sum_recv):
    per, groups, rows, channels, width, planes, disp_count, row_count = dims
    total = planes * disp_count
    hid_rows = rows + 2
    block = rows * groups
    hslab = hid_rows * channels
    half_rows = hid_rows // 2
    half_hslab = half_rows * channels
    cost_planes = planes + 4
    chunks = block // CHUNK
    disp = lax.axis_index("disp")
    row = lax.axis_index("rows")
    odd = lax.rem(row, 2)
    half = lax.rem(disp, 2)
    other_core = disp + 1 - 2 * half
    partner = row + 1 - 2 * odd
    target = row + 2 - 4 * odd
    source = row - 2 + 4 * odd
    has_target = (target >= 0) & (target < row_count)
    has_source = (source >= 0) & (source < row_count)
    first_plane = disp * planes
    base = first_plane - 2

    load1 = pltpu.make_async_copy(k1_hbm, k1_ref, load_sems.at[0])
    load2 = pltpu.make_async_copy(k2_hbm, k2_ref, load_sems.at[1])
    load3 = pltpu.make_async_copy(proj_hbm, proj_ref, load_sems.at[2])
    load1.start()
    load2.start()
    load3.start()

    barrier = pltpu.get_barrier_semaphore()

    def greet(d, r):
        pl.semaphore_signal(barrier, inc=1, device_id=(d, r), device_id_type=MESH)

    greet(disp, partner)
    for step in range(1, disp_count):
        greet(lax.rem(disp + step, disp_count), row)

    @pl.when(has_source)
    def _():
        greet(disp, source)

    pl.semaphore_wait(barrier, disp_count + has_target.astype(jnp.int32))

    part = per // PIECES

    def copy(kind, q, src, dst, device):
        k, piece = divmod(q, PIECES)
        at, chans = pl.ds(k * CHUNK, CHUNK), pl.ds(piece * part, part)
        return pltpu.make_async_remote_copy(
            src_ref=src.at[chans, at, :],
            dst_ref=dst.at[half, chans, at, :],
            send_sem=send_sems.at[kind, q],
            recv_sem=recv_sems.at[kind, q],
            device_id=device,
            device_id_type=MESH,
        )

    def to_partner(k, src=left_ref):
        return copy(0, k, src, pair, (disp, partner))

    def pair_to_core(k):
        return copy(1, k, pair.at[half], pair, (other_core, row))

    def pair_to_target(k):
        return copy(2, k, pair.at[half], far, (disp, target))

    def far_to_core(k):
        return copy(3, k, far.at[half], far, (other_core, row))

    for side, src in enumerate((left_ref, right_ref)):
        @pl.when(half == side)
        def _():
            for q in range(chunks * PIECES):
                to_partner(q, src).start()

    def forward_pair(k):
        for q in range(k * PIECES, (k + 1) * PIECES):
            to_partner(q).wait_recv()

            @pl.when(has_target)
            def _():
                pair_to_target(q).start()

            pair_to_core(q).start()

    def forward_far(k):
        @pl.when(has_source)
        def _():
            for q in range(k * PIECES, (k + 1) * PIECES):
                pair_to_target(q).wait_recv()
                far_to_core(q).start()

    lane = lax.broadcasted_iota(jnp.int32, (CHUNK, width), 1)
    for d in range(cost_planes):
        plane = base + d
        keep = (lane >= plane) & (plane >= 0) & (plane < total)
        inside[d] = jnp.where(keep, 1.0 / per, 0.0).astype(jnp.bfloat16)

    gap = lax.broadcasted_iota(jnp.int32, (width, width), 1) - lax.broadcasted_iota(jnp.int32, (width, width), 0)
    for d1 in range(INNER):
        by = base + d1
        hit = (gap == by) | (gap == by - width) | (gap == by + width)
        shifts[d1] = jnp.where(hit, 1.0, 0.0).astype(jnp.bfloat16)

    def correlate(lref, rref, cost, k, buf, kind=jnp.bfloat16):
        at = pl.ds(k * CHUNK, CHUNK)
        right = rref[:, at, :].reshape(per * CHUNK, width)
        for d1 in range(INNER):
            moved = jnp.dot(right, shifts[d1], preferred_element_type=jnp.float32)
            shifted[buf, d1] = moved.astype(jnp.bfloat16).reshape(per, CHUNK, width)
        for d2 in range(cost_planes // INNER):
            back = d2 * INNER
            left = []
            for j in range(per):
                value = lref[j, at, :]
                value = pltpu.roll(value, width - back, 1) if back else value
                left.append(value.astype(kind))
            for d1 in range(INNER):
                terms = [left[j] * shifted[buf, d1, j].astype(kind) for j in range(per)]
                while len(terms) > 1:
                    terms = [x + y for x, y in zip(terms[::2], terms[1::2])]
                acc = terms[0].astype(jnp.bfloat16)
                acc = pltpu.roll(acc, back, 1) if back else acc
                cost[pl.ds((back + d1) * block + k * CHUNK, CHUNK), :] = acc * inside[back + d1]

    def correlate_own(k):
        correlate(left_ref, right_ref, cost_own, k, k % 2, jnp.float32)

    def correlate_pair(k):
        for q in range(k * PIECES, (k + 1) * PIECES):
            pair_to_core(q).wait_recv()
        correlate(pair.at[0], pair.at[1], cost_pair, k, 0)

    def wait_far(k):
        @pl.when(has_source)
        def _():
            far_to_core(k).wait_recv()

    def correlate_far(k):
        correlate(far.at[0], far.at[1], cost_far, k, 1)

    @pl.when(jnp.logical_not(has_source))
    def _():
        far[...] = jnp.zeros_like(far)

    for k in range(chunks):
        correlate_own(k)

    def weights():
        w1[...] = jnp.zeros_like(w1)
        w2[...] = jnp.zeros_like(w2)
        load1.wait()
        load2.wait()
        load3.wait()
        for a in range(3):
            for b in range(3):
                for e in range(3):
                    tap = k1_ref[a, b, e]
                    for y in range(half_rows):
                        at = (e * half_rows + y) * channels
                        which, within = divmod(y + a, rows)
                        to = b * block + within * groups
                        for v in range(2):
                            lo = to + (which + v) % 2 * 3 * block
                            w1[v, at:at + channels, lo:lo + groups] = tap
                    tap = k2_ref[a, b, e]
                    for pd in range(2):
                        for y in range(rows):
                            at = ((e * 2 + pd) * rows + y) * channels
                            to = (b + pd) * hslab + (y + a) * channels
                            w2[at:at + channels, to:to + channels] = tap

    hlane = lax.broadcasted_iota(jnp.int32, (half_hslab, width), 1)
    top = jnp.where(row > 0, 1.0, 0.0)
    bottom = jnp.where(row < row_count - 1, 1.0, 0.0)

    def first(p, low, other):
        at = pl.ds(pl.multiple_of(p * block, CHUNK), 3 * block)
        z = jnp.concatenate([cost_own[at, :], other[at, :]], axis=0)
        z = jnp.dot(w1[1 - low], z, preferred_element_type=jnp.float32)
        h = jnp.maximum(sum_taps(z, half_hslab, hlane, width), 0.0)
        plane = p + first_plane - 1
        valid = jnp.where((plane >= 0) & (plane < total), 1.0, 0.0)
        for y in range(half_rows):
            edge = valid
            if y == 0:
                edge = edge * jnp.where(low == 0, top, 1.0)
            if y == half_rows - 1:
                edge = edge * jnp.where(low == 1, bottom, 1.0)
            at = pl.ds(pl.multiple_of(p * hslab + low * half_hslab + y * channels, CHUNK), channels)
            hidden[at, :] = (h[y * channels:(y + 1) * channels] * edge).astype(jnp.bfloat16)

    def first_planes(begin, end, low, other):
        def one_plane(p, carry):
            first(p, low, other)
            return carry

        lax.fori_loop(begin, end, one_plane, 0, unroll=end - begin)

    for k in range(chunks):
        forward_pair(k)
        if k == 0:
            weights()
        else:
            correlate_pair(k - 1)
    forward_far(0)
    correlate_pair(chunks - 1)
    forward_far(1)
    steps = chunks - 1
    cuts = [(planes + 2) * i // steps for i in range(steps + 1)]
    for i in range(steps):
        wait_far(i)
        first_planes(cuts[i], cuts[i + 1], 1 - odd, cost_pair)
        correlate_far(i)
        if i + 2 < chunks:
            forward_far(i + 2)
    wait_far(chunks - 1)
    correlate_far(chunks - 1)
    first_planes(0, planes + 2, odd, cost_far)

    m2 = rows * channels
    olane = lax.broadcasted_iota(jnp.int32, (2 * m2, width), 1)
    diagonal = lax.broadcasted_iota(jnp.int32, (channels, channels), 0) == lax.broadcasted_iota(
        jnp.int32, (channels, channels), 1)
    proj = jnp.sum(jnp.where(diagonal, proj_ref[...], 0.0), axis=1, keepdims=True)

    def second(t, carry):
        at = pl.ds(pl.multiple_of(t * 2 * hslab, CHUNK), 4 * hslab)
        z = jnp.dot(w2[...], hidden[at, :], preferred_element_type=jnp.float32)
        out = jnp.maximum(sum_taps(z, 2 * m2, olane, width), 0.0)
        for pd in range(2):
            start = pl.multiple_of((t * 2 + pd + 1) * hslab + channels, CHUNK)
            for y in range(rows):
                centre = hidden[pl.ds(start + y * channels, channels), :].astype(jnp.float32)
                lo = pd * m2 + y * channels
                refined = (out[lo:lo + channels] + centre) * proj
                logits_ref[y, pl.ds(t * 2 + pd, 1), :] = jnp.sum(refined, axis=0, keepdims=True)
        return carry

    lax.fori_loop(0, planes // 2, second, 0, unroll=planes // 2)

    weights_now = jnp.exp(logits_ref[...])
    ids = lax.broadcasted_iota(jnp.int32, weights_now.shape, 1) + first_plane
    sums[disp, 0] = jnp.sum(weights_now, axis=1)
    sums[disp, 1] = jnp.sum(weights_now * ids.astype(jnp.float32), axis=1)

    def share(step):
        return pltpu.make_async_remote_copy(
            src_ref=sums.at[disp],
            dst_ref=sums.at[disp],
            send_sem=sum_send.at[step],
            recv_sem=sum_recv.at[step],
            device_id=(lax.rem(disp + step, disp_count), row),
            device_id_type=MESH,
        )

    for step in range(1, disp_count):
        share(step).start()
    for k in range(chunks * PIECES):
        to_partner(k).wait_send()
        pair_to_core(k).wait_send()

        @pl.when(has_target)
        def _():
            pair_to_target(k).wait_send()

        @pl.when(has_source)
        def _():
            far_to_core(k).wait_send()

    for step in range(1, disp_count):
        share(step).wait()
    both = sums[0]
    for d in range(1, disp_count):
        both = both + sums[d]
    disparity_ref[...] = both[1] / both[0] / total


def emit(logits_in, disparity_in, logits_out, disparity_out):
    logits_out[...] = logits_in[...]
    disparity_out[...] = disparity_in[...]


def per_device(left_features, right_features, conv_first, conv_second, projection):
    disp_count = lax.axis_size("disp")
    row_count = lax.axis_size("rows")
    planes = DPL_DEV
    features, rows, width = left_features.shape
    channels, groups = conv_first.shape[:2]
    per = features // groups

    def arrange(v):
        return v.reshape(groups, per, rows, width).transpose(1, 2, 0, 3).reshape(per, rows * groups, width)

    left, right = arrange(left_features), arrange(right_features)
    both = (2,) + left.shape
    def in_hbm(v):
        return pltpu.with_memory_space_constraint(v, pltpu.HBM)

    k1 = in_hbm(conv_first.transpose(2, 3, 4, 0, 1))
    k2 = in_hbm(conv_second.transpose(2, 3, 4, 0, 1))
    proj = in_hbm(projection[None])
    hid_rows = rows + 2
    block, hslab = rows * groups, hid_rows * channels
    chunks = block // CHUNK
    dims = (per, groups, rows, channels, width, planes, disp_count, row_count)
    vmem = pl.BlockSpec(memory_space=pltpu.VMEM)
    hbm = pl.BlockSpec(memory_space=pltpu.HBM)
    results = (
        jax.ShapeDtypeStruct((rows, planes, width), jnp.float32),
        jax.ShapeDtypeStruct((rows, width), jnp.float32),
    )
    made = pl.pallas_call(
        functools.partial(body, dims),
        out_shape=results,
        in_specs=[vmem, vmem, hbm, hbm, hbm],
        out_specs=(vmem, vmem),
        scratch_shapes=[
            pltpu.VMEM(k1.shape, k1.dtype),
            pltpu.VMEM(k2.shape, k2.dtype),
            pltpu.VMEM(proj.shape, proj.dtype),
            pltpu.VMEM(both, left.dtype),
            pltpu.VMEM(both, left.dtype),
            pltpu.VMEM(((planes + 4) * block, width), jnp.bfloat16),
            pltpu.VMEM(((planes + 4) * block, width), jnp.bfloat16),
            pltpu.VMEM(((planes + 4) * block, width), jnp.bfloat16),
            pltpu.VMEM(((planes + 2) * hslab, width), jnp.bfloat16),
            pltpu.VMEM((2, INNER, per, CHUNK, width), jnp.bfloat16),
            pltpu.VMEM((INNER, width, width), jnp.bfloat16),
            pltpu.VMEM((planes + 4, CHUNK, width), jnp.bfloat16),
            pltpu.VMEM((2, 3 * hid_rows // 2 * channels, 6 * block), jnp.bfloat16),
            pltpu.VMEM((3 * 2 * rows * channels, 4 * hslab), jnp.bfloat16),
            pltpu.VMEM((disp_count, 2, rows, width), jnp.float32),
            pltpu.SemaphoreType.DMA((3,)),
            pltpu.SemaphoreType.DMA((4, chunks * PIECES)),
            pltpu.SemaphoreType.DMA((4, chunks * PIECES)),
            pltpu.SemaphoreType.DMA((disp_count,)),
            pltpu.SemaphoreType.DMA((disp_count,)),
        ],
        compiler_params=pltpu.CompilerParams(
            collective_id=0, has_side_effects=True, vmem_limit_bytes=VMEM_BYTES),
    )(left, right, k1, k2, proj)
    return pl.pallas_call(
        emit,
        out_shape=results,
        in_specs=[vmem, vmem],
        out_specs=(vmem, vmem),
        compiler_params=pltpu.CompilerParams(vmem_limit_bytes=VMEM_BYTES // 8),
    )(*made)


def solution(mesh):
    return jax.shard_map(
        per_device,
        mesh=mesh,
        in_specs=(P(None, "rows", None), P(None, "rows", None), P(), P(), P()),
        out_specs=(P("rows", "disp", None), P("rows", None)),
        check_vma=False,
    )
```

```python
import functools

import jax
import jax.numpy as jnp
from jax import lax
from jax.experimental import pallas as pl
from jax.experimental.pallas import tpu as pltpu
from jax.sharding import PartitionSpec as P

DPL_DEV = 24
HALO = 2
INNER = 7
CHUNK = 16
PIECES = 1
VMEM_BYTES = 28 << 20
MESH = pl.DeviceIdType.MESH


def sum_taps(z, m, lane, width):
    low = jnp.where(lane == 0, 0.0, pltpu.roll(z[:m], 1, 1))
    high = jnp.where(lane == width - 1, 0.0, pltpu.roll(z[2 * m:], width - 1, 1))
    return low + z[m:2 * m] + high


def body(dims, left_ref, right_ref, k1_hbm, k2_hbm, proj_hbm, logits_ref, disparity_ref,
         k1_ref, k2_ref, proj_ref, pair, far, cost_own, cost_pair, cost_far, hidden, shifted, shifts, inside, w1, w2, sums,
         load_sems, send_sems, recv_sems, sum_send, sum_recv):
    per, groups, rows, channels, width, planes, disp_count, row_count = dims
    total = planes * disp_count
    hid_rows = rows + 2
    block = rows * groups
    hslab = hid_rows * channels
    half_rows = hid_rows // 2
    half_hslab = half_rows * channels
    cost_planes = planes + 4
    chunks = block // CHUNK
    disp = lax.axis_index("disp")
    row = lax.axis_index("rows")
    odd = lax.rem(row, 2)
    half = lax.rem(disp, 2)
    other_core = disp + 1 - 2 * half
    partner = row + 1 - 2 * odd
    target = row + 2 - 4 * odd
    source = row - 2 + 4 * odd
    has_target = (target >= 0) & (target < row_count)
    has_source = (source >= 0) & (source < row_count)
    first_plane = disp * planes
    base = first_plane - 2

    load1 = pltpu.make_async_copy(k1_hbm, k1_ref, load_sems.at[0])
    load2 = pltpu.make_async_copy(k2_hbm, k2_ref, load_sems.at[1])
    load3 = pltpu.make_async_copy(proj_hbm, proj_ref, load_sems.at[2])
    load1.start()
    load2.start()
    load3.start()

    barrier = pltpu.get_barrier_semaphore()

    def greet(d, r):
        pl.semaphore_signal(barrier, inc=1, device_id=(d, r), device_id_type=MESH)

    greet(disp, partner)
    for step in range(1, disp_count):
        greet(lax.rem(disp + step, disp_count), row)

    @pl.when(has_source)
    def _():
        greet(disp, source)

    pl.semaphore_wait(barrier, disp_count + has_target.astype(jnp.int32))

    part = per // PIECES

    def copy(kind, q, src, dst, device):
        k, piece = divmod(q, PIECES)
        at, chans = pl.ds(k * CHUNK, CHUNK), pl.ds(piece * part, part)
        return pltpu.make_async_remote_copy(
            src_ref=src.at[chans, at, :],
            dst_ref=dst.at[half, chans, at, :],
            send_sem=send_sems.at[kind, q],
            recv_sem=recv_sems.at[kind, q],
            device_id=device,
            device_id_type=MESH,
        )

    def to_partner(k, src=left_ref):
        return copy(0, k, src, pair, (disp, partner))

    def pair_to_core(k):
        return copy(1, k, pair.at[half], pair, (other_core, row))

    def pair_to_target(k):
        return copy(2, k, pair.at[half], far, (disp, target))

    def far_to_core(k):
        return copy(3, k, far.at[half], far, (other_core, row))

    for side, src in enumerate((left_ref, right_ref)):
        @pl.when(half == side)
        def _():
            for q in range(chunks * PIECES):
                to_partner(q, src).start()

    def forward_pair(k):
        for q in range(k * PIECES, (k + 1) * PIECES):
            to_partner(q).wait_recv()

            @pl.when(has_target)
            def _():
                pair_to_target(q).start()

            pair_to_core(q).start()

    def forward_far(k):
        @pl.when(has_source)
        def _():
            for q in range(k * PIECES, (k + 1) * PIECES):
                pair_to_target(q).wait_recv()
                far_to_core(q).start()

    lane = lax.broadcasted_iota(jnp.int32, (CHUNK, width), 1)
    for d in range(cost_planes):
        plane = base + d
        keep = (lane >= plane) & (plane >= 0) & (plane < total)
        inside[d] = jnp.where(keep, 1.0 / per, 0.0).astype(jnp.bfloat16)

    gap = lax.broadcasted_iota(jnp.int32, (width, width), 1) - lax.broadcasted_iota(jnp.int32, (width, width), 0)
    for d1 in range(INNER):
        by = base + d1
        hit = (gap == by) | (gap == by - width) | (gap == by + width)
        shifts[d1] = jnp.where(hit, 1.0, 0.0).astype(jnp.bfloat16)

    def correlate(lref, rref, cost, k, buf, kind=jnp.bfloat16):
        at = pl.ds(k * CHUNK, CHUNK)
        right = rref[:, at, :].reshape(per * CHUNK, width)
        for d1 in range(INNER):
            moved = jnp.dot(right, shifts[d1], preferred_element_type=jnp.float32)
            shifted[buf, d1] = moved.astype(jnp.bfloat16).reshape(per, CHUNK, width)
        for d2 in range(cost_planes // INNER):
            back = d2 * INNER
            left = []
            for j in range(per):
                value = lref[j, at, :]
                value = pltpu.roll(value, width - back, 1) if back else value
                left.append(value.astype(kind))
            for d1 in range(INNER):
                terms = [left[j] * shifted[buf, d1, j].astype(kind) for j in range(per)]
                while len(terms) > 1:
                    terms = [x + y for x, y in zip(terms[::2], terms[1::2])]
                acc = terms[0].astype(jnp.bfloat16)
                acc = pltpu.roll(acc, back, 1) if back else acc
                cost[pl.ds((back + d1) * block + k * CHUNK, CHUNK), :] = acc * inside[back + d1]

    def correlate_own(k):
        correlate(left_ref, right_ref, cost_own, k, k % 2, jnp.float32)

    def correlate_pair(k):
        for q in range(k * PIECES, (k + 1) * PIECES):
            pair_to_core(q).wait_recv()
        correlate(pair.at[0], pair.at[1], cost_pair, k, 0)

    def wait_far(k):
        @pl.when(has_source)
        def _():
            for q in range(k * PIECES, (k + 1) * PIECES):
                far_to_core(q).wait_recv()

    def correlate_far(k):
        correlate(far.at[0], far.at[1], cost_far, k, 1)

    @pl.when(jnp.logical_not(has_source))
    def _():
        far[...] = jnp.zeros_like(far)

    for k in range(chunks):
        correlate_own(k)

    def weights():
        w1[...] = jnp.zeros_like(w1)
        w2[...] = jnp.zeros_like(w2)
        load1.wait()
        load2.wait()
        load3.wait()
        for a in range(3):
            for b in range(3):
                for e in range(3):
                    tap = k1_ref[a, b, e]
                    for y in range(half_rows):
                        at = (e * half_rows + y) * channels
                        which, within = divmod(y + a, rows)
                        to = b * block + within * groups
                        for v in range(2):
                            lo = to + (which + v) % 2 * 3 * block
                            w1[v, at:at + channels, lo:lo + groups] = tap
                    tap = k2_ref[a, b, e]
                    for pd in range(2):
                        for y in range(rows):
                            at = ((e * 2 + pd) * rows + y) * channels
                            to = (b + pd) * hslab + (y + a) * channels
                            w2[at:at + channels, to:to + channels] = tap

    hlane = lax.broadcasted_iota(jnp.int32, (half_hslab, width), 1)
    top = jnp.where(row > 0, 1.0, 0.0)
    bottom = jnp.where(row < row_count - 1, 1.0, 0.0)

    def first(p, low, other):
        at = pl.ds(pl.multiple_of(p * block, CHUNK), 3 * block)
        z = jnp.concatenate([cost_own[at, :], other[at, :]], axis=0)
        z = jnp.dot(w1[1 - low], z, preferred_element_type=jnp.float32)
        h = jnp.maximum(sum_taps(z, half_hslab, hlane, width), 0.0)
        plane = p + first_plane - 1
        valid = jnp.where((plane >= 0) & (plane < total), 1.0, 0.0)
        for y in range(half_rows):
            edge = valid
            if y == 0:
                edge = edge * jnp.where(low == 0, top, 1.0)
            if y == half_rows - 1:
                edge = edge * jnp.where(low == 1, bottom, 1.0)
            at = pl.ds(pl.multiple_of(p * hslab + low * half_hslab + y * channels, CHUNK), channels)
            hidden[at, :] = (h[y * channels:(y + 1) * channels] * edge).astype(jnp.bfloat16)

    def first_planes(begin, end, low, other):
        def one_plane(p, carry):
            first(p, low, other)
            return carry

        lax.fori_loop(begin, end, one_plane, 0, unroll=end - begin)

    for k in range(chunks):
        forward_pair(k)
        if k == 0:
            weights()
        elif k < chunks - 1:
            correlate_pair(k - 1)
    forward_far(0)
    correlate_pair(chunks - 2)
    correlate_pair(chunks - 1)
    forward_far(1)
    steps = chunks - 1
    cuts = [(planes + 2) * i // steps for i in range(steps + 1)]
    for i in range(steps):
        wait_far(i)
        first_planes(cuts[i], cuts[i + 1], 1 - odd, cost_pair)
        correlate_far(i)
        if i + 2 < chunks:
            forward_far(i + 2)
    wait_far(chunks - 1)
    correlate_far(chunks - 1)
    first_planes(0, planes + 2, odd, cost_far)

    m2 = rows * channels
    olane = lax.broadcasted_iota(jnp.int32, (2 * m2, width), 1)
    diagonal = lax.broadcasted_iota(jnp.int32, (channels, channels), 0) == lax.broadcasted_iota(
        jnp.int32, (channels, channels), 1)
    proj = jnp.sum(jnp.where(diagonal, proj_ref[...], 0.0), axis=1, keepdims=True)

    def second(t, carry):
        at = pl.ds(pl.multiple_of(t * 2 * hslab, CHUNK), 4 * hslab)
        z = jnp.dot(w2[...], hidden[at, :], preferred_element_type=jnp.float32)
        out = jnp.maximum(sum_taps(z, 2 * m2, olane, width), 0.0)
        for pd in range(2):
            start = pl.multiple_of((t * 2 + pd + 1) * hslab + channels, CHUNK)
            for y in range(rows):
                centre = hidden[pl.ds(start + y * channels, channels), :].astype(jnp.float32)
                lo = pd * m2 + y * channels
                refined = (out[lo:lo + channels] + centre) * proj
                logits_ref[y, pl.ds(t * 2 + pd, 1), :] = jnp.sum(refined, axis=0, keepdims=True)
        return carry

    lax.fori_loop(0, planes // 2, second, 0, unroll=planes // 2)

    weights_now = jnp.exp(logits_ref[...])
    ids = lax.broadcasted_iota(jnp.int32, weights_now.shape, 1) + first_plane
    sums[disp, 0] = jnp.sum(weights_now, axis=1)
    sums[disp, 1] = jnp.sum(weights_now * ids.astype(jnp.float32), axis=1)

    def share(step):
        return pltpu.make_async_remote_copy(
            src_ref=sums.at[disp],
            dst_ref=sums.at[disp],
            send_sem=sum_send.at[step],
            recv_sem=sum_recv.at[step],
            device_id=(lax.rem(disp + step, disp_count), row),
            device_id_type=MESH,
        )

    for step in range(1, disp_count):
        share(step).start()
    for k in range(chunks * PIECES):
        to_partner(k).wait_send()
        pair_to_core(k).wait_send()

        @pl.when(has_target)
        def _():
            pair_to_target(k).wait_send()

        @pl.when(has_source)
        def _():
            far_to_core(k).wait_send()

    for step in range(1, disp_count):
        share(step).wait()
    both = sums[0]
    for d in range(1, disp_count):
        both = both + sums[d]
    disparity_ref[...] = both[1] / both[0] / total


def emit(logits_in, disparity_in, logits_out, disparity_out):
    logits_out[...] = logits_in[...]
    disparity_out[...] = disparity_in[...]


def per_device(left_features, right_features, conv_first, conv_second, projection):
    disp_count = lax.axis_size("disp")
    row_count = lax.axis_size("rows")
    planes = DPL_DEV
    features, rows, width = left_features.shape
    channels, groups = conv_first.shape[:2]
    per = features // groups

    def arrange(v):
        return v.reshape(groups, per, rows, width).transpose(1, 2, 0, 3).reshape(per, rows * groups, width)

    left, right = arrange(left_features), arrange(right_features)
    both = (2,) + left.shape
    def in_hbm(v):
        return pltpu.with_memory_space_constraint(v, pltpu.HBM)

    k1 = in_hbm(conv_first.transpose(2, 3, 4, 0, 1))
    k2 = in_hbm(conv_second.transpose(2, 3, 4, 0, 1))
    proj = in_hbm(projection[None])
    hid_rows = rows + 2
    block, hslab = rows * groups, hid_rows * channels
    chunks = block // CHUNK
    dims = (per, groups, rows, channels, width, planes, disp_count, row_count)
    vmem = pl.BlockSpec(memory_space=pltpu.VMEM)
    hbm = pl.BlockSpec(memory_space=pltpu.HBM)
    results = (
        jax.ShapeDtypeStruct((rows, planes, width), jnp.float32),
        jax.ShapeDtypeStruct((rows, width), jnp.float32),
    )
    made = pl.pallas_call(
        functools.partial(body, dims),
        out_shape=results,
        in_specs=[vmem, vmem, hbm, hbm, hbm],
        out_specs=(vmem, vmem),
        scratch_shapes=[
            pltpu.VMEM(k1.shape, k1.dtype),
            pltpu.VMEM(k2.shape, k2.dtype),
            pltpu.VMEM(proj.shape, proj.dtype),
            pltpu.VMEM(both, left.dtype),
            pltpu.VMEM(both, left.dtype),
            pltpu.VMEM(((planes + 4) * block, width), jnp.bfloat16),
            pltpu.VMEM(((planes + 4) * block, width), jnp.bfloat16),
            pltpu.VMEM(((planes + 4) * block, width), jnp.bfloat16),
            pltpu.VMEM(((planes + 2) * hslab, width), jnp.bfloat16),
            pltpu.VMEM((2, INNER, per, CHUNK, width), jnp.bfloat16),
            pltpu.VMEM((INNER, width, width), jnp.bfloat16),
            pltpu.VMEM((planes + 4, CHUNK, width), jnp.bfloat16),
            pltpu.VMEM((2, 3 * hid_rows // 2 * channels, 6 * block), jnp.bfloat16),
            pltpu.VMEM((3 * 2 * rows * channels, 4 * hslab), jnp.bfloat16),
            pltpu.VMEM((disp_count, 2, rows, width), jnp.float32),
            pltpu.SemaphoreType.DMA((3,)),
            pltpu.SemaphoreType.DMA((4, chunks * PIECES)),
            pltpu.SemaphoreType.DMA((4, chunks * PIECES)),
            pltpu.SemaphoreType.DMA((disp_count,)),
            pltpu.SemaphoreType.DMA((disp_count,)),
        ],
        compiler_params=pltpu.CompilerParams(
            collective_id=0, has_side_effects=True, vmem_limit_bytes=VMEM_BYTES),
    )(left, right, k1, k2, proj)
    return pl.pallas_call(
        emit,
        out_shape=results,
        in_specs=[vmem, vmem],
        out_specs=(vmem, vmem),
        compiler_params=pltpu.CompilerParams(vmem_limit_bytes=VMEM_BYTES // 8),
    )(*made)


def solution(mesh):
    return jax.shard_map(
        per_device,
        mesh=mesh,
        in_specs=(P(None, "rows", None), P(None, "rows", None), P(), P(), P()),
        out_specs=(P("rows", "disp", None), P("rows", None)),
        check_vma=False,
    )
```

```python
import functools

import jax
import jax.numpy as jnp
from jax import lax
from jax.experimental import pallas as pl
from jax.experimental.pallas import tpu as pltpu
from jax.sharding import PartitionSpec as P

DPL_DEV = 24
HALO = 2
INNER = 7
CHUNK = 16
PIECES = 1
VMEM_BYTES = 28 << 20
MESH = pl.DeviceIdType.MESH


def sum_taps(z, m, lane, width):
    low = jnp.where(lane == 0, 0.0, pltpu.roll(z[:m], 1, 1))
    high = jnp.where(lane == width - 1, 0.0, pltpu.roll(z[2 * m:], width - 1, 1))
    return low + z[m:2 * m] + high


def body(dims, left_ref, right_ref, k1_hbm, k2_hbm, proj_hbm, logits_ref, disparity_ref,
         k1_ref, k2_ref, proj_ref, pair, far, cost_own, cost_pair, cost_far, hidden, shifted, shifts, inside, w1, w2, sums,
         load_sems, send_sems, recv_sems, sum_send, sum_recv):
    per, groups, rows, channels, width, planes, disp_count, row_count = dims
    total = planes * disp_count
    hid_rows = rows + 2
    block = rows * groups
    hslab = hid_rows * channels
    half_rows = hid_rows // 2
    half_hslab = half_rows * channels
    cost_planes = planes + 4
    chunks = block // CHUNK
    disp = lax.axis_index("disp")
    row = lax.axis_index("rows")
    odd = lax.rem(row, 2)
    half = lax.rem(disp, 2)
    other_core = disp + 1 - 2 * half
    partner = row + 1 - 2 * odd
    target = row + 2 - 4 * odd
    source = row - 2 + 4 * odd
    has_target = (target >= 0) & (target < row_count)
    has_source = (source >= 0) & (source < row_count)
    first_plane = disp * planes
    base = first_plane - 2

    load1 = pltpu.make_async_copy(k1_hbm, k1_ref, load_sems.at[0])
    load2 = pltpu.make_async_copy(k2_hbm, k2_ref, load_sems.at[1])
    load3 = pltpu.make_async_copy(proj_hbm, proj_ref, load_sems.at[2])

    barrier = pltpu.get_barrier_semaphore()

    def greet(d, r):
        pl.semaphore_signal(barrier, inc=1, device_id=(d, r), device_id_type=MESH)

    greet(disp, partner)
    for step in range(1, disp_count):
        greet(lax.rem(disp + step, disp_count), row)

    @pl.when(has_source)
    def _():
        greet(disp, source)

    pl.semaphore_wait(barrier, disp_count + has_target.astype(jnp.int32))

    part = per // PIECES

    def copy(kind, q, src, dst, device):
        k, piece = divmod(q, PIECES)
        at, chans = pl.ds(k * CHUNK, CHUNK), pl.ds(piece * part, part)
        return pltpu.make_async_remote_copy(
            src_ref=src.at[chans, at, :],
            dst_ref=dst.at[half, chans, at, :],
            send_sem=send_sems.at[kind, q],
            recv_sem=recv_sems.at[kind, q],
            device_id=device,
            device_id_type=MESH,
        )

    def to_partner(k, src=left_ref):
        return copy(0, k, src, pair, (disp, partner))

    def pair_to_core(k):
        return copy(1, k, pair.at[half], pair, (other_core, row))

    def pair_to_target(k):
        return copy(2, k, pair.at[half], far, (disp, target))

    def far_to_core(k):
        return copy(3, k, far.at[half], far, (other_core, row))

    for side, src in enumerate((left_ref, right_ref)):
        @pl.when(half == side)
        def _():
            for q in range(chunks * PIECES):
                to_partner(q, src).start()

    load1.start()
    load2.start()
    load3.start()

    def forward_pair(k):
        for q in range(k * PIECES, (k + 1) * PIECES):
            to_partner(q).wait_recv()

            @pl.when(has_target)
            def _():
                pair_to_target(q).start()

            pair_to_core(q).start()

    def forward_far(k):
        @pl.when(has_source)
        def _():
            for q in range(k * PIECES, (k + 1) * PIECES):
                pair_to_target(q).wait_recv()
                far_to_core(q).start()

    lane = lax.broadcasted_iota(jnp.int32, (CHUNK, width), 1)
    for d in range(cost_planes):
        plane = base + d
        keep = (lane >= plane) & (plane >= 0) & (plane < total)
        inside[d] = jnp.where(keep, 1.0 / per, 0.0).astype(jnp.bfloat16)

    gap = lax.broadcasted_iota(jnp.int32, (width, width), 1) - lax.broadcasted_iota(jnp.int32, (width, width), 0)
    for d1 in range(INNER):
        by = base + d1
        hit = (gap == by) | (gap == by - width) | (gap == by + width)
        shifts[d1] = jnp.where(hit, 1.0, 0.0).astype(jnp.bfloat16)

    def correlate(lref, rref, cost, k, buf, kind=jnp.bfloat16):
        at = pl.ds(k * CHUNK, CHUNK)
        right = rref[:, at, :].reshape(per * CHUNK, width)
        for d1 in range(INNER):
            moved = jnp.dot(right, shifts[d1], preferred_element_type=jnp.float32)
            shifted[buf, d1] = moved.astype(jnp.bfloat16).reshape(per, CHUNK, width)
        for d2 in range(cost_planes // INNER):
            back = d2 * INNER
            left = []
            for j in range(per):
                value = lref[j, at, :]
                value = pltpu.roll(value, width - back, 1) if back else value
                left.append(value.astype(kind))
            for d1 in range(INNER):
                terms = [left[j] * shifted[buf, d1, j].astype(kind) for j in range(per)]
                while len(terms) > 1:
                    terms = [x + y for x, y in zip(terms[::2], terms[1::2])]
                acc = terms[0].astype(jnp.bfloat16)
                acc = pltpu.roll(acc, back, 1) if back else acc
                cost[pl.ds((back + d1) * block + k * CHUNK, CHUNK), :] = acc * inside[back + d1]

    def correlate_own(k):
        correlate(left_ref, right_ref, cost_own, k, k % 2, jnp.float32)

    def correlate_pair(k):
        for q in range(k * PIECES, (k + 1) * PIECES):
            pair_to_core(q).wait_recv()
        correlate(pair.at[0], pair.at[1], cost_pair, k, 0)

    def wait_far(k):
        @pl.when(has_source)
        def _():
            for q in range(k * PIECES, (k + 1) * PIECES):
                far_to_core(q).wait_recv()

    def correlate_far(k):
        correlate(far.at[0], far.at[1], cost_far, k, 1)

    @pl.when(jnp.logical_not(has_source))
    def _():
        far[...] = jnp.zeros_like(far)

    for k in range(chunks):
        correlate_own(k)

    def weights():
        w1[...] = jnp.zeros_like(w1)
        w2[...] = jnp.zeros_like(w2)
        load1.wait()
        load2.wait()
        load3.wait()
        for a in range(3):
            for b in range(3):
                for e in range(3):
                    tap = k1_ref[a, b, e]
                    for y in range(half_rows):
                        at = (e * half_rows + y) * channels
                        which, within = divmod(y + a, rows)
                        to = b * block + within * groups
                        for v in range(2):
                            lo = to + (which + v) % 2 * 3 * block
                            w1[v, at:at + channels, lo:lo + groups] = tap
                    tap = k2_ref[a, b, e]
                    for pd in range(2):
                        for y in range(rows):
                            at = ((e * 2 + pd) * rows + y) * channels
                            to = (b + pd) * hslab + (y + a) * channels
                            w2[at:at + channels, to:to + channels] = tap

    hlane = lax.broadcasted_iota(jnp.int32, (half_hslab, width), 1)
    top = jnp.where(row > 0, 1.0, 0.0)
    bottom = jnp.where(row < row_count - 1, 1.0, 0.0)

    def first(p, low, other):
        at = pl.ds(pl.multiple_of(p * block, CHUNK), 3 * block)
        z = jnp.concatenate([cost_own[at, :], other[at, :]], axis=0)
        z = jnp.dot(w1[1 - low], z, preferred_element_type=jnp.float32)
        h = jnp.maximum(sum_taps(z, half_hslab, hlane, width), 0.0)
        plane = p + first_plane - 1
        valid = jnp.where((plane >= 0) & (plane < total), 1.0, 0.0)
        for y in range(half_rows):
            edge = valid
            if y == 0:
                edge = edge * jnp.where(low == 0, top, 1.0)
            if y == half_rows - 1:
                edge = edge * jnp.where(low == 1, bottom, 1.0)
            at = pl.ds(pl.multiple_of(p * hslab + low * half_hslab + y * channels, CHUNK), channels)
            hidden[at, :] = (h[y * channels:(y + 1) * channels] * edge).astype(jnp.bfloat16)

    def first_planes(begin, end, low, other):
        def one_plane(p, carry):
            first(p, low, other)
            return carry

        lax.fori_loop(begin, end, one_plane, 0, unroll=end - begin)

    for k in range(chunks):
        forward_pair(k)
        if k == 0:
            weights()
        elif k < chunks - 1:
            correlate_pair(k - 1)
    forward_far(0)
    correlate_pair(chunks - 2)
    correlate_pair(chunks - 1)
    forward_far(1)
    steps = chunks - 1
    cuts = [(planes + 2) * i // steps for i in range(steps + 1)]
    for i in range(steps):
        wait_far(i)
        first_planes(cuts[i], cuts[i + 1], 1 - odd, cost_pair)
        correlate_far(i)
        if i + 2 < chunks:
            forward_far(i + 2)
    wait_far(chunks - 1)
    correlate_far(chunks - 1)
    first_planes(0, planes + 2, odd, cost_far)

    m2 = rows * channels
    olane = lax.broadcasted_iota(jnp.int32, (2 * m2, width), 1)
    diagonal = lax.broadcasted_iota(jnp.int32, (channels, channels), 0) == lax.broadcasted_iota(
        jnp.int32, (channels, channels), 1)
    proj = jnp.sum(jnp.where(diagonal, proj_ref[...], 0.0), axis=1, keepdims=True)

    def second(t, carry):
        at = pl.ds(pl.multiple_of(t * 2 * hslab, CHUNK), 4 * hslab)
        z = jnp.dot(w2[...], hidden[at, :], preferred_element_type=jnp.float32)
        out = jnp.maximum(sum_taps(z, 2 * m2, olane, width), 0.0)
        for pd in range(2):
            start = pl.multiple_of((t * 2 + pd + 1) * hslab + channels, CHUNK)
            for y in range(rows):
                centre = hidden[pl.ds(start + y * channels, channels), :].astype(jnp.float32)
                lo = pd * m2 + y * channels
                refined = (out[lo:lo + channels] + centre) * proj
                logits_ref[y, pl.ds(t * 2 + pd, 1), :] = jnp.sum(refined, axis=0, keepdims=True)
        return carry

    lax.fori_loop(0, planes // 2, second, 0, unroll=planes // 2)

    weights_now = jnp.exp(logits_ref[...])
    ids = lax.broadcasted_iota(jnp.int32, weights_now.shape, 1) + first_plane
    sums[disp, 0] = jnp.sum(weights_now, axis=1)
    sums[disp, 1] = jnp.sum(weights_now * ids.astype(jnp.float32), axis=1)

    def share(step):
        return pltpu.make_async_remote_copy(
            src_ref=sums.at[disp],
            dst_ref=sums.at[disp],
            send_sem=sum_send.at[step],
            recv_sem=sum_recv.at[step],
            device_id=(lax.rem(disp + step, disp_count), row),
            device_id_type=MESH,
        )

    for step in range(1, disp_count):
        share(step).start()
    for k in range(chunks * PIECES):
        to_partner(k).wait_send()
        pair_to_core(k).wait_send()

        @pl.when(has_target)
        def _():
            pair_to_target(k).wait_send()

        @pl.when(has_source)
        def _():
            far_to_core(k).wait_send()

    for step in range(1, disp_count):
        share(step).wait()
    both = sums[0]
    for d in range(1, disp_count):
        both = both + sums[d]
    disparity_ref[...] = both[1] / both[0] / total


def emit(logits_in, disparity_in, logits_out, disparity_out):
    logits_out[...] = logits_in[...]
    disparity_out[...] = disparity_in[...]


def per_device(left_features, right_features, conv_first, conv_second, projection):
    disp_count = lax.axis_size("disp")
    row_count = lax.axis_size("rows")
    planes = DPL_DEV
    features, rows, width = left_features.shape
    channels, groups = conv_first.shape[:2]
    per = features // groups

    def arrange(v):
        return v.reshape(groups, per, rows, width).transpose(1, 2, 0, 3).reshape(per, rows * groups, width)

    left, right = arrange(left_features), arrange(right_features)
    both = (2,) + left.shape
    def in_hbm(v):
        return pltpu.with_memory_space_constraint(v, pltpu.HBM)

    k1 = in_hbm(conv_first.transpose(2, 3, 4, 0, 1))
    k2 = in_hbm(conv_second.transpose(2, 3, 4, 0, 1))
    proj = in_hbm(projection[None])
    hid_rows = rows + 2
    block, hslab = rows * groups, hid_rows * channels
    chunks = block // CHUNK
    dims = (per, groups, rows, channels, width, planes, disp_count, row_count)
    vmem = pl.BlockSpec(memory_space=pltpu.VMEM)
    hbm = pl.BlockSpec(memory_space=pltpu.HBM)
    results = (
        jax.ShapeDtypeStruct((rows, planes, width), jnp.float32),
        jax.ShapeDtypeStruct((rows, width), jnp.float32),
    )
    made = pl.pallas_call(
        functools.partial(body, dims),
        out_shape=results,
        in_specs=[vmem, vmem, hbm, hbm, hbm],
        out_specs=(vmem, vmem),
        scratch_shapes=[
            pltpu.VMEM(k1.shape, k1.dtype),
            pltpu.VMEM(k2.shape, k2.dtype),
            pltpu.VMEM(proj.shape, proj.dtype),
            pltpu.VMEM(both, left.dtype),
            pltpu.VMEM(both, left.dtype),
            pltpu.VMEM(((planes + 4) * block, width), jnp.bfloat16),
            pltpu.VMEM(((planes + 4) * block, width), jnp.bfloat16),
            pltpu.VMEM(((planes + 4) * block, width), jnp.bfloat16),
            pltpu.VMEM(((planes + 2) * hslab, width), jnp.bfloat16),
            pltpu.VMEM((2, INNER, per, CHUNK, width), jnp.bfloat16),
            pltpu.VMEM((INNER, width, width), jnp.bfloat16),
            pltpu.VMEM((planes + 4, CHUNK, width), jnp.bfloat16),
            pltpu.VMEM((2, 3 * hid_rows // 2 * channels, 6 * block), jnp.bfloat16),
            pltpu.VMEM((3 * 2 * rows * channels, 4 * hslab), jnp.bfloat16),
            pltpu.VMEM((disp_count, 2, rows, width), jnp.float32),
            pltpu.SemaphoreType.DMA((3,)),
            pltpu.SemaphoreType.DMA((4, chunks * PIECES)),
            pltpu.SemaphoreType.DMA((4, chunks * PIECES)),
            pltpu.SemaphoreType.DMA((disp_count,)),
            pltpu.SemaphoreType.DMA((disp_count,)),
        ],
        compiler_params=pltpu.CompilerParams(
            collective_id=0, has_side_effects=True, vmem_limit_bytes=VMEM_BYTES),
    )(left, right, k1, k2, proj)
    return pl.pallas_call(
        emit,
        out_shape=results,
        in_specs=[vmem, vmem],
        out_specs=(vmem, vmem),
        compiler_params=pltpu.CompilerParams(vmem_limit_bytes=VMEM_BYTES // 8),
    )(*made)


def solution(mesh):
    return jax.shard_map(
        per_device,
        mesh=mesh,
        in_specs=(P(None, "rows", None), P(None, "rows", None), P(), P(), P()),
        out_specs=(P("rows", "disp", None), P("rows", None)),
        check_vma=False,
    )
```
